32 devices in a mesh: ctx: 16 (over z, y, x), head: 2 (over core).
Axes of the slice: x: 2, y: 2, z: 4, core: 2. Of those that a mesh axis runs over, the one named last changes fastest.
Arguments:
- queries: bfloat16 [8192, 4, 4, 128], P('ctx', 'head')
- keys: bfloat16 [8192, 4, 128], P('ctx')
- values: bfloat16 [8192, 4, 128], P('ctx'), may hold values from -6 to 6
- output_gradient: bfloat16 [8192, 4, 4, 128], P('ctx', 'head'), may hold values from -6 to 6
- selected: int32 [16, 2], replicated, may hold values from 0 to 14, as said below
Outputs:
- attn_out: bfloat16 [8192, 4, 4, 128], P('ctx', 'head')
- grad_q: bfloat16 [8192, 4, 4, 128], P('ctx', 'head')
- grad_k: bfloat16 [8192, 4, 128], P('ctx', 'head')
- grad_v: bfloat16 [8192, 4, 128], P('ctx', 'head')
The draws below stay inside these ranges and needn't reach their ends.
Inputs may be any that keep to these rules, and one draw needn't show every extreme that they name: selected[b, j] <= b for every block b; an entry equal to b selects no block; for b >= 2 the two entries of a row differ and both are below b.
All inputs are finite; a program needn't handle non-finite values.
Results may differ from the reference program's by a relative error of at most 0.011.
Values may be sent and summed in bfloat16 or wider, within the bound.
A program may use at most 128 MiB of HBM per device.

```python
import jax
import jax.numpy as jnp
from jax import lax

KEY_VALUE_HEADS = 4
QUERY_PER_KEY = 4
HEAD_DIMENSION = 128
BLK = 512
NB = 16
SEQUENCE_TOKENS = 8192


def draw_keys(key, part):
    return jnp.clip(jax.random.normal(jax.random.fold_in(key, 11), (SEQUENCE_TOKENS, KEY_VALUE_HEADS, HEAD_DIMENSION), jnp.float32), -6.0, 6.0).astype(jnp.bfloat16)


def draw_queries(key, part):
    return jnp.clip(jax.random.normal(jax.random.fold_in(key, 12), (SEQUENCE_TOKENS, QUERY_PER_KEY, KEY_VALUE_HEADS, HEAD_DIMENSION), jnp.float32), -6.0, 6.0).astype(jnp.bfloat16)


def draw_selected(key, part):
    index = jnp.arange(NB, dtype=jnp.int32)
    hottest = jax.random.randint(jax.random.fold_in(key, 1), (), 0, NB // 4)
    coin_flip = jax.random.randint(jax.random.fold_in(key, 2), (NB,), 0, 2)
    first_pick = jax.random.randint(jax.random.fold_in(key, 3), (NB,), 0, jnp.maximum(index, 1))
    first_pick = jnp.where((coin_flip == 1) & (index > hottest), hottest, first_pick)
    other_pick = jax.random.randint(jax.random.fold_in(key, 4), (NB,), 0, jnp.maximum(index - 1, 1))
    second_pick = other_pick + (other_pick >= first_pick).astype(jnp.int32)
    second_pick = jnp.where(index == 0, 0, second_pick)
    first_pick = jnp.where(index == NB - 1, hottest, first_pick)
    second_pick = jnp.where(index == NB - 1, NB - 2, second_pick)
    return jnp.stack([first_pick, second_pick], axis=1).astype(jnp.int32)


def steps_of(rng, dims, shards, low, high):
    def one(axis_at, parts):
        heights = jax.random.uniform(jax.random.fold_in(jax.random.fold_in(rng, 6), axis_at), (parts,), jnp.float32, low / len(shards), high / len(shards))
        return jnp.repeat(jnp.exp(heights), dims[axis_at] // parts).reshape((-1,) + (1,) * (len(dims) - axis_at - 1))

    factor_of = one(*shards[0])
    for cut in shards[1:]:
        factor_of = factor_of * one(*cut)
    return factor_of


def normal_values(own_key, dims, deviation, limit, cuts=(), kind=jnp.bfloat16):
    drawn = jax.random.normal(own_key, dims, jnp.float32) * deviation
    if len(cuts) > 0:
        drawn = steps_of(own_key, dims, cuts, -0.22, 0.18) * drawn
    return jnp.clip(drawn, min=-limit, max=limit).astype(kind)


def setup_inputs(seed: int = 0) -> dict:
    streams_of = jax.random.split(jax.random.key(seed), 6)
    return {
        "queries": draw_queries(jax.random.fold_in(streams_of[5], 71), 0),
        "keys": draw_keys(jax.random.fold_in(streams_of[5], 71), 0),
        "values": normal_values(streams_of[2], (SEQUENCE_TOKENS, KEY_VALUE_HEADS, HEAD_DIMENSION), 1.0, 6.0, ((0, 16),)),
        "output_gradient": normal_values(streams_of[3], (SEQUENCE_TOKENS, QUERY_PER_KEY, KEY_VALUE_HEADS, HEAD_DIMENSION), 1.0, 6.0, ((0, 16), (1, 2))),
        "selected": draw_selected(jax.random.fold_in(streams_of[5], 71), 0),
    }


def attend_block(block_q, block_k, block_v, block_g, visible, softmax_scale):
    query_f = block_q.astype(jnp.float32)
    key_f = block_k.astype(jnp.float32)
    value_f = block_v.astype(jnp.float32)
    grad_f = block_g.astype(jnp.float32)
    scores = jnp.einsum("qgnd,knd->gnqk", query_f, key_f) * softmax_scale
    scores = jnp.where(visible, scores, -jnp.inf)
    row_max = jnp.max(scores, axis=-1, keepdims=True)
    weights = jnp.exp(scores - row_max)
    probs = weights / jnp.sum(weights, axis=-1, keepdims=True)
    probs_low = probs.astype(jnp.bfloat16)
    block_out = jnp.einsum("gnqk,knd->qgnd", probs_low.astype(jnp.float32), value_f).astype(jnp.bfloat16)
    row_dot = jnp.sum(grad_f * block_out.astype(jnp.float32), axis=-1)
    grad_probs = jnp.einsum("qgnd,knd->gnqk", grad_f, value_f)
    grad_scores = (probs * (grad_probs - jnp.transpose(row_dot, (1, 2, 0))[..., None]) * softmax_scale).astype(jnp.bfloat16)
    block_dq = jnp.einsum("gnqk,knd->qgnd", grad_scores.astype(jnp.float32), key_f).astype(jnp.bfloat16)
    part_k = jnp.einsum("gnqk,qgnd->knd", grad_scores.astype(jnp.float32), query_f)
    part_v = jnp.einsum("gnqk,qgnd->knd", probs_low.astype(jnp.float32), grad_f)
    return block_out, block_dq, part_k, part_v


def reference(queries, keys, values, output_gradient, selected):
    softmax_scale = HEAD_DIMENSION ** -0.5
    position = jnp.arange(BLK, dtype=jnp.int32)
    causal = position[:, None] >= position[None, :]

    def block_rows(source, block_id):
        return lax.dynamic_slice_in_dim(source, (block_id * BLK).astype(jnp.int32), BLK, 0)

    def one_block(totals, block_id):
        grad_keys, grad_values = totals
        first_pick = selected[block_id, 0]
        second_pick = selected[block_id, 1]
        chosen_blocks = [first_pick, second_pick, block_id]
        block_k = jnp.concatenate([block_rows(keys, chosen) for chosen in chosen_blocks], axis=0)
        block_v = jnp.concatenate([block_rows(values, chosen) for chosen in chosen_blocks], axis=0)
        visible = jnp.concatenate([jnp.broadcast_to(first_pick < block_id, (BLK, BLK)), jnp.broadcast_to(second_pick < block_id, (BLK, BLK)), causal], axis=1)
        block_out, block_dq, part_k, part_v = attend_block(block_rows(queries, block_id), block_k, block_v, block_rows(output_gradient, block_id), visible, softmax_scale)
        for column, chosen in enumerate(chosen_blocks):
            start_row = (chosen * BLK).astype(jnp.int32)
            grad_keys = lax.dynamic_update_slice_in_dim(grad_keys, block_rows(grad_keys, chosen) + part_k[column * BLK:(column + 1) * BLK], start_row, 0)
            grad_values = lax.dynamic_update_slice_in_dim(grad_values, block_rows(grad_values, chosen) + part_v[column * BLK:(column + 1) * BLK], start_row, 0)
        return (grad_keys, grad_values), (block_out, block_dq)

    empty_grads = jnp.zeros(keys.shape, jnp.float32)
    (grad_keys, grad_values), (all_out, all_dq) = lax.scan(one_block, (empty_grads, empty_grads), jnp.arange(NB, dtype=jnp.int32))
    return (all_out.reshape(queries.shape), all_dq.reshape(queries.shape), grad_keys.astype(jnp.bfloat16), grad_values.astype(jnp.bfloat16))
```

```python
import functools
import math

import jax
import jax.numpy as jnp
from jax import lax
from jax.experimental import pallas as pl
from jax.experimental.pallas import tpu as pltpu
from jax.sharding import PartitionSpec as P

F32 = jnp.float32
BF16 = jnp.bfloat16
CHUNKS = 2


def dot_nn(a, b):
    return lax.dot_general(a, b, (((1,), (0,)), ((), ())), preferred_element_type=F32)


def greet(blocks, halves):
    me, half = lax.axis_index("ctx"), lax.axis_index("head")
    barrier = pltpu.get_barrier_semaphore()

    @pl.loop(1, blocks)
    def _(i):
        pl.semaphore_signal(barrier, inc=1, device_id={"ctx": lax.rem(me + i, blocks), "head": half})

    for i in range(1, halves):
        pl.semaphore_signal(barrier, inc=1, device_id={"ctx": me, "head": lax.rem(half + i, halves)})
    pl.semaphore_wait(barrier, blocks - 1 + halves - 1)


def flip(x):
    return x.astype(F32).T.astype(BF16)


def step_kernel(blocks, halves, sel_ref, kv_ref, own_ref, q_ref, do_ref, grads_ref, oo_ref, dqo_ref,
                qv, dov, qt, dot, near, send, ks, vs, kt, vt, probs, dots, dqt, dk, dv, dko, dvo, down, outv, dqv,
                dnear, arrived, home, ret,
                s1, r1, s2, r2, xs, xr, xl, b1, c1, b2, c2, ys, yr, yl, *held):
    me, half = lax.axis_index("ctx"), lax.axis_index("head")
    heads, group, rows, size = qv.shape
    part = group // halves
    side_blocks, piece = kv_ref.shape[1], kv_ref.shape[2]
    units = heads * CHUNKS
    keys = rows // CHUNKS
    tile = rows // 2
    side, col = me // side_blocks, lax.rem(me, side_blocks)
    base = side * side_blocks
    lower, upper = side == 0, side > 0
    scale = size ** -0.5
    factor = scale * math.log2(math.e)
    visible = [sel_ref[me, j] < me for j in range(2)]
    here = {"ctx": me, "head": half}
    greet(blocks, halves)

    def near_all(make):
        @pl.loop(1, side_blocks)
        def _(i):
            make(lax.rem(col + i, side_blocks)).start()

    def far_all(make):
        @pl.loop(0, side_blocks)
        def _(i):
            make(lax.rem(col + i, side_blocks)).start()

    def scatter(u, first):
        return lambda d: pltpu.make_async_remote_copy(
            kv_ref.at[u, d], held[u].at[me], s1.at[u], r1.at[u], device_id={"ctx": first + d, "head": half})

    for u in range(units):
        @pl.when(lower)
        def _(u=u):
            far_all(scatter(u, side_blocks))

        near_all(scatter(u, base))

    moves = []
    for e, (src, dst) in enumerate(((q_ref, qv), (do_ref, dov))):
        place = dst.at[:, pl.ds(half * part, part)]
        for i in range(1, halves):
            other = lax.rem(half + i, halves)
            moves.append(pltpu.make_async_remote_copy(
                src.at[pl.ds(other * heads, heads)], place, xs.at[e, i - 1], xr.at[e, i - 1],
                device_id={"ctx": me, "head": other}))
        moves.append(pltpu.make_async_copy(src.at[pl.ds(half * heads, heads)], place, xl.at[e]))
    for move in moves:
        move.start()

    def fetch_first(u, count):
        span = pl.ds(0, count)
        return pltpu.make_async_remote_copy(
            held[u].at[span], held[u].at[span], s1.at[u], r1.at[u], device_id=here)

    def fetch_last(u):
        span = pl.ds(0, side_blocks - 1)
        return pltpu.make_async_remote_copy(
            send.at[u, span], near.at[u, :, span], s2.at[u], r2.at[u], device_id=here)

    def relay(u):
        held[u][me] = kv_ref[u, col]

        @pl.when(lower)
        def _():
            fetch_first(u, side_blocks - 1).wait_recv()

        @pl.when(upper)
        def _():
            fetch_first(u, blocks - 1).wait_recv()

        @pl.loop(0, side_blocks)
        def _(d):
            for j in range(2):
                send[u, d, j] = held[u][sel_ref[base + d, j]]

        near_all(lambda d: pltpu.make_async_remote_copy(
            send.at[u, d], near.at[u, :, col], s2.at[u], r2.at[u], device_id={"ctx": base + d, "head": half}))
        for j in range(2):
            near[u, j, col] = held[u][sel_ref[me, j]]

    def back_first(u):
        span = pl.ds(0, side_blocks - 1)
        return pltpu.make_async_remote_copy(
            dnear.at[u, :, span], arrived.at[u, span], b1.at[u], c1.at[u], device_id=here)

    def back_last(u, count):
        span = pl.ds(0, count)
        return pltpu.make_async_remote_copy(
            home.at[u, span], home.at[u, span], b2.at[u], c2.at[u], device_id=here)

    together = math.gcd(4, side_blocks)

    def collect(u):
        back_first(u).wait_recv()

        def total_of(s, first):
            def add(c, total):
                for k in range(together):
                    d = c * together + k
                    b = base + d
                    for j in range(2):
                        mine = ((sel_ref[b, j] == s) & (b > s)).astype(F32)
                        total = total + arrived[u, d, j].astype(F32) * mine
                return total

            total = lax.fori_loop(first, side_blocks // together, add, jnp.zeros((piece, size), F32))
            home[u, s] = total.astype(BF16)

        def deliver(s):
            pltpu.make_async_remote_copy(
                home.at[u, s], ret.at[u, side, col], b2.at[u], c2.at[u],
                device_id={"ctx": s, "head": half}).start()

        @pl.when(upper)
        def _():
            @pl.loop(0, side_blocks)
            def _(i):
                total_of(lax.rem(col + i, side_blocks), 0)

                @pl.when(i > 0)
                def _():
                    deliver(lax.rem(col + i - 1, side_blocks))

            deliver(lax.rem(col + side_blocks - 1, side_blocks))

        @pl.loop(1, side_blocks + 1)
        def _(i):
            d = lax.rem(col + i, side_blocks)
            total_of(base + d, (d + 1) // together)

            @pl.when(i > 1)
            def _():
                deliver(base + lax.rem(col + i - 1, side_blocks))

        ret[u, side, col] = home[u, me]

    def results(n, e):
        src, dst = ((outv, oo_ref), (dqv, dqo_ref))[e]
        made = []
        place = dst.at[half * heads + n]
        for i in range(1, halves):
            other = lax.rem(half + i, halves)
            made.append(pltpu.make_async_remote_copy(
                src.at[n, pl.ds(other * part, part)], place, ys.at[n, e, i - 1], yr.at[n, e, i - 1],
                device_id={"ctx": me, "head": other}))
        made.append(pltpu.make_async_copy(src.at[n, pl.ds(half * part, part)], place, yl.at[n, e]))
        return made

    def join(x):
        if piece % 16 == 0:
            return x.reshape(keys, size)
        return x.astype(F32).reshape(keys, size).astype(BF16)

    pieces = side_blocks // 2

    def place_keys(n, j, k, key, value):
        ks[n, j, k * keys:(k + 1) * keys] = key
        vs[n, j, k * keys:(k + 1) * keys] = value
        kt[n, j, k] = flip(key)
        vt[n, :, j * rows + k * keys:j * rows + (k + 1) * keys] = flip(value)

    def outputs(n, g):
        for t in range(2):
            span = slice(t * tile, (t + 1) * tile)
            counts = (rows, rows, (t + 1) * tile)
            q_t = qt[n, g, :, span]
            scores, tops = [], []
            for j in range(3):
                s = dot_nn(ks[n, j, 0:counts[j], :], q_t) * factor
                if j == 2:
                    key_at = lax.broadcasted_iota(jnp.int32, s.shape, 0)
                    query_at = lax.broadcasted_iota(jnp.int32, s.shape, 1) + t * tile
                    s = jnp.where(key_at <= query_at, s, -jnp.inf)
                top = jnp.max(s, axis=0, keepdims=True)
                if j < 2:
                    top = jnp.where(visible[j], top, -jnp.inf)
                scores.append(s)
                tops.append(top)
            top = jnp.maximum(jnp.maximum(tops[0], tops[1]), tops[2])
            total = jnp.zeros_like(top)
            weights = []
            for j in range(3):
                shift = jnp.where(visible[j], top, jnp.inf) if j < 2 else top
                e = jnp.exp2(scores[j] - shift)
                total = total + jnp.sum(e, axis=0, keepdims=True)
                weights.append(e)
            inverse = 1.0 / total
            out_t = jnp.zeros((size, tile), F32)
            for j in range(3):
                low = (weights[j] * inverse).astype(BF16)
                probs[n, g, j * rows:j * rows + counts[j], span] = low
                out_t = out_t + dot_nn(vt[n, :, j * rows:j * rows + counts[j]], low)
            out_low = out_t.astype(BF16).astype(F32)
            dots[n, g, :, span] = jnp.sum(dot[n, g, :, span].astype(F32) * out_low, axis=0, keepdims=True)
            outv[n, g, span, :] = out_low.T.astype(BF16)

    def gradients(n, g, low, key_t, value, span, dk_at, dv_at):
        dp = dot_nn(value, dot[n, g, :, span])
        ds = (low.astype(F32) * (dp - dots[n, g, :, span])).astype(BF16)
        dk_at[...] += dot_nn(ds, qv[n, g, span, :])
        dv_at[...] += dot_nn(low, dov[n, g, span, :])
        return dot_nn(key_t, ds)

    def chunk(n, k, g):
        every = slice(0, rows)
        total = jnp.zeros((size, rows), F32)
        for j in range(2):
            at = pl.multiple_of(k * keys, keys)
            low = probs[n, g, pl.ds(pl.multiple_of(j * rows + k * keys, keys), keys), :]
            total = total + gradients(n, g, low, kt[n, j, k], vs[n, j, pl.ds(at, keys), :], every,
                                      dk.at[j], dv.at[j])

        @pl.when(k == 0)
        def _():
            dqt[n, g] = total

        @pl.when(k > 0)
        def _():
            dqt[n, g] += total

    def own_chunk(n, g):
        total = dqt[n, g]
        tails = []
        for k in range(CHUNKS):
            span = slice(k * keys, rows)
            low = probs[n, g, 2 * rows + k * keys:2 * rows + (k + 1) * keys, span]
            at = slice(k * keys, (k + 1) * keys)
            tails.append(gradients(n, g, low, kt[n, 2, k], vs[n, 2, at, :], span, dko.at[at], dvo.at[at]))
        for t in range(CHUNKS):
            span = slice(t * keys, (t + 1) * keys)
            dq = total[:, span]
            for k in range(t + 1):
                dq = dq + tails[k][:, (t - k) * keys:(t - k + 1) * keys]
            dqv[n, g, span, :] = (dq * scale).T.astype(BF16)

    for n in range(heads):
        for k in range(CHUNKS):
            span = slice(k * keys, (k + 1) * keys)
            place_keys(n, 2, k, own_ref[n, 0, span], own_ref[n, 1, span])

    for move in moves:
        move.wait()

    @pl.loop(0, heads * group)
    def _(at):
        n, g = at // group, lax.rem(at, group)
        qt[n, g] = flip(qv[n, g])
        dot[n, g] = flip(dov[n, g])

    for u in range(CHUNKS):
        relay(u)

    @pl.loop(0, heads)
    def _(n):
        for k in range(CHUNKS):
            u = n * CHUNKS + k
            fetch_last(u).wait_recv()
            for j in range(2):
                place_keys(n, j, k, join(near[u, j, 0:pieces]), join(near[u, j, pieces:2 * pieces]))

        @pl.loop(0, group)
        def _(g):
            outputs(n, g)
            for m in range(1, heads):
                for k in range(CHUNKS):
                    @pl.when((n == m - 1) & (g == k * (group - 1)))
                    def _(m=m, k=k):
                        relay(m * CHUNKS + k)

            @pl.when((n > 0) & (lax.rem(g, 2) == 1))
            def _():
                collect((n - 1) * CHUNKS + g // 2)

        for move in results(n, 0):
            move.start()

        @pl.loop(0, CHUNKS * group)
        def _(at):
            k, g = at // group, lax.rem(at, group)
            u = n * CHUNKS + k

            @pl.when(g == 0)
            def _():
                dk[...] = jnp.zeros_like(dk)
                dv[...] = jnp.zeros_like(dv)

            chunk(n, k, g)

            @pl.when(g == group - 1)
            def _():
                for j in range(2):
                    dnear[u, j, 0:pieces] = (dk[j] * scale).reshape(pieces, piece, size).astype(BF16)
                    dnear[u, j, pieces:2 * pieces] = dv[j].reshape(pieces, piece, size).astype(BF16)
                near_all(lambda d: pltpu.make_async_remote_copy(
                    dnear.at[u, :, d], arrived.at[u, col], b1.at[u], c1.at[u],
                    device_id={"ctx": base + d, "head": half}))
                for j in range(2):
                    arrived[u, col, j] = dnear[u, j, col]

    @pl.loop(0, heads * group)
    def _(at):
        n, g = at // group, lax.rem(at, group)

        @pl.when(g == 0)
        def _():
            dko[...] = jnp.zeros_like(dko)
            dvo[...] = jnp.zeros_like(dvo)

        own_chunk(n, g)

        for k in range(CHUNKS):
            @pl.when(at == (1 + 4 * k))
            def _(k=k):
                collect((heads - 1) * CHUNKS + k)

        @pl.when(g == group - 1)
        def _():
            for k in range(CHUNKS):
                u = n * CHUNKS + k
                span = slice(k * keys, (k + 1) * keys)
                down[u, 0:pieces] = (dko[span] * scale).reshape(pieces, piece, size)
                down[u, pieces:2 * pieces] = dvo[span].reshape(pieces, piece, size)
            for move in results(n, 1):
                move.start()

    for u in range(units):
        fetch_last(u).wait_send()
        back_first(u).wait_send()
    for n in range(heads):
        for e in range(2):
            for move in results(n, e):
                move.wait()

    @pl.when(lower)
    def _():
        for u in range(units):
            fetch_first(u, blocks - 1).wait_send()
            back_last(u, side_blocks - 1).wait_send()
            back_last(u, blocks - 1).wait_recv()
            grads_ref[u] = (ret[u, 1].astype(F32) + ret[u, 0].astype(F32) + down[u]).astype(BF16)

    @pl.when(upper)
    def _():
        for u in range(units):
            fetch_first(u, side_blocks - 1).wait_send()
            back_last(u, blocks - 1).wait_send()
            back_last(u, side_blocks - 1).wait_recv()
            grads_ref[u] = (ret[u, 1].astype(F32) + down[u]).astype(BF16)


def step(selected, kv, own, q, do, blocks, halves):
    units, side_blocks, piece, size = kv.shape
    heads = units // CHUNKS
    full, part, rows, _ = q.shape
    group = part * halves
    keys = rows // CHUNKS
    near = pl.BlockSpec(memory_space=pltpu.VMEM)
    far = pl.BlockSpec(memory_space=pl.ANY)
    dma = pltpu.SemaphoreType.DMA
    vmem = pltpu.VMEM
    return pl.pallas_call(
        functools.partial(step_kernel, blocks, halves),
        in_specs=[pl.BlockSpec(memory_space=pltpu.SMEM), near, near, far, far],
        out_specs=[near, far, far],
        out_shape=[jax.ShapeDtypeStruct(kv.shape, BF16), jax.ShapeDtypeStruct(q.shape, BF16),
                   jax.ShapeDtypeStruct(q.shape, BF16)],
        scratch_shapes=[
            vmem((heads, group, rows, size), BF16),
            vmem((heads, group, rows, size), BF16),
            vmem((heads, group, size, rows), BF16),
            vmem((heads, group, size, rows), BF16),
            vmem((units, 2, side_blocks, piece, size), BF16),
            vmem((units, side_blocks, 2, piece, size), BF16),
            vmem((heads, 3, rows, size), BF16),
            vmem((heads, 3, rows, size), BF16),
            vmem((heads, 3, CHUNKS, size, keys), BF16),
            vmem((heads, size, 3 * rows), BF16),
            vmem((heads, group, 3 * rows, rows), BF16),
            vmem((heads, group, 1, rows), F32),
            vmem((heads, group, size, rows), F32),
            vmem((2, keys, size), F32),
            vmem((2, keys, size), F32),
            vmem((rows, size), F32),
            vmem((rows, size), F32),
            vmem((units, side_blocks, piece, size), F32),
            vmem((heads, group, rows, size), BF16),
            vmem((heads, group, rows, size), BF16),
            vmem((units, 2, side_blocks, piece, size), BF16),
            vmem((units, side_blocks, 2, piece, size), BF16),
            vmem((units, blocks, piece, size), BF16),
            vmem((units, 2, side_blocks, piece, size), BF16),
            dma((units,)), dma((units,)), dma((units,)), dma((units,)),
            dma((2, halves - 1)), dma((2, halves - 1)), dma((2,)),
            dma((units,)), dma((units,)), dma((units,)), dma((units,)),
            dma((heads, 2, halves - 1)), dma((heads, 2, halves - 1)), dma((heads, 2)),
        ] + [vmem((blocks, piece, size), BF16)] * units,
        compiler_params=pltpu.CompilerParams(collective_id=0, has_side_effects=True,
                                             vmem_limit_bytes=56 * 2**20),
    )(selected, kv, own, q, do)


def on_device(queries, keys, values, output_gradient, selected):
    rows, kv_count, size = keys.shape
    blocks, halves = lax.axis_size("ctx"), lax.axis_size("head")
    own_heads = kv_count // halves
    half = lax.axis_index("head")
    side_blocks = blocks // 2
    piece = 2 * rows // (CHUNKS * side_blocks)
    own = jnp.stack([keys, values])
    own = lax.dynamic_slice_in_dim(own, half * own_heads, own_heads, 2)
    own = jnp.transpose(own, (2, 0, 1, 3))
    cut = own.reshape(own_heads, 2, CHUNKS, rows // CHUNKS, size)
    cut = jnp.transpose(cut, (0, 2, 1, 3, 4)).reshape(own_heads * CHUNKS, side_blocks, piece, size)
    q, do = jnp.transpose(queries, (2, 1, 0, 3)), jnp.transpose(output_gradient, (2, 1, 0, 3))
    grads, out, dq = step(selected, cut, own, q, do, blocks, halves)
    grads = grads.reshape(own_heads, CHUNKS, 2, rows // CHUNKS, size)
    grads = jnp.transpose(grads, (2, 1, 3, 0, 4)).reshape(2, rows, own_heads, size)
    return jnp.transpose(out, (2, 1, 0, 3)), jnp.transpose(dq, (2, 1, 0, 3)), grads[0], grads[1]


def solution(mesh):
    return jax.shard_map(
        on_device,
        mesh=mesh,
        in_specs=(
            P("ctx", "head", None, None),
            P("ctx", None, None),
            P("ctx", None, None),
            P("ctx", "head", None, None),
            P(),
        ),
        out_specs=(
            P("ctx", "head", None, None),
            P("ctx", "head", None, None),
            P("ctx", "head", None),
            P("ctx", "head", None),
        ),
        check_vma=False,
    )
```

```python
import functools
import math

import jax
import jax.numpy as jnp
from jax import lax
from jax.experimental import pallas as pl
from jax.experimental.pallas import tpu as pltpu
from jax.sharding import PartitionSpec as P

F32 = jnp.float32
BF16 = jnp.bfloat16
CHUNKS = 2
EXTRA = 16
TILE = 256


def dot_nn(a, b):
    return lax.dot_general(a, b, (((1,), (0,)), ((), ())), preferred_element_type=F32)


def greet(blocks, halves):
    me, half = lax.axis_index("ctx"), lax.axis_index("head")
    barrier = pltpu.get_barrier_semaphore()

    @pl.loop(1, blocks)
    def _(i):
        pl.semaphore_signal(barrier, inc=1, device_id={"ctx": lax.rem(me + i, blocks), "head": half})

    for i in range(1, halves):
        pl.semaphore_signal(barrier, inc=1, device_id={"ctx": me, "head": lax.rem(half + i, halves)})
    return lambda: pl.semaphore_wait(barrier, blocks - 1 + halves - 1)


def pick(shape, column_of):
    row = lax.broadcasted_iota(jnp.int32, shape, 0)
    column = lax.broadcasted_iota(jnp.int32, shape, 1)
    return jnp.where(column == column_of(row), 1.0, 0.0).astype(BF16)


def split(x, size):
    bits = size.bit_length() - 1
    assert size == 1 << bits
    return lax.shift_right_logical(x, bits), lax.bitwise_and(x, size - 1)


def flip(x):
    return x.astype(F32).T.astype(BF16)


def step_kernel(blocks, halves, sel_ref, k_ref, v_ref, q_ref, do_ref, oo_ref, dqo_ref, gk_ref, gv_ref,
                kv_raw, raw, staged, own_ref, kv_ref, perm, back, qv, dov, qt, dot, near, send, ks, vs, kt, vt, marks, peaks, probs, dots, dqt, dk, dv, dko, dvo, down, outv, dqv, landed,
                dnear, arrived, home, ret,
                s1, r1, s2, r2, kl, ql, ol, xs, xr, xl, b1, c1, b2, c2, ys, yr, yl, *held):
    me, half = lax.axis_index("ctx"), lax.axis_index("head")
    heads, group, rows, size = qv.shape
    part = group // halves
    side_blocks, piece = kv_ref.shape[1], kv_ref.shape[2]
    units = heads * CHUNKS
    keys = rows // CHUNKS
    tile = rows // 2
    side, col = me // side_blocks, lax.rem(me, side_blocks)
    base = side * side_blocks
    lower, upper = side == 0, side > 0
    scale = size ** -0.5
    factor = scale * math.log2(math.e)
    visible = [sel_ref[j, me] < me for j in range(2)]
    here = {"ctx": me, "head": half}
    kv_heads = staged.shape[1]
    joined = greet(blocks, halves)

    loads = [pltpu.make_async_copy(src, kv_raw.at[e], kl.at[e]) for e, src in enumerate((k_ref, v_ref))]
    reads = [pltpu.make_async_copy(src, raw.at[e], ql.at[e]) for e, src in enumerate((q_ref, do_ref))]
    for copy in loads + reads:
        copy.start()

    kv_tokens = TILE // kv_heads
    tokens = TILE // (kv_heads * part)
    grad_tokens = TILE // heads

    def kv_column(row):
        h, t = split(row, kv_tokens)
        return t * kv_heads + half * heads + h

    def q_column(row):
        slab, t = split(row, tokens)
        n, g = split(slab, part)
        return t * (part * kv_heads) + g * kv_heads + n

    def q_back(row):
        t, slab = split(row, part * kv_heads)
        g, n = split(slab, kv_heads)
        return (n * part + g) * tokens + t

    def grad_back(row):
        t, h = split(row, heads)
        return h * grad_tokens + t

    choose = pick((heads * kv_tokens, TILE), kv_column)
    vt[:, size:size + EXTRA, :] = jnp.ones((heads, EXTRA, 3 * rows), BF16)
    for copy in loads:
        copy.wait()
    for e in range(2):
        for i in range(rows // kv_tokens):
            y = dot_nn(choose, kv_raw[e, i * TILE:(i + 1) * TILE, :]).astype(BF16)
            for h in range(heads):
                own_ref[h, e, i * kv_tokens:(i + 1) * kv_tokens] = y[h * kv_tokens:(h + 1) * kv_tokens]
    pieces = side_blocks // 2

    def cut(x):
        if piece % 16 == 0:
            return x.reshape(pieces, piece, size)
        return x.astype(F32).reshape(pieces, piece, size).astype(BF16)

    for n in range(heads):
        for k in range(CHUNKS):
            for e in range(2):
                kv_ref[n * CHUNKS + k, e * pieces:(e + 1) * pieces] = cut(own_ref[n, e, k * keys:(k + 1) * keys])
    joined()

    def near_all(make):
        @pl.loop(1, side_blocks)
        def _(i):
            make(lax.rem(col + i, side_blocks)).start()

    def far_all(make):
        @pl.loop(0, side_blocks)
        def _(i):
            make(lax.rem(col + i, side_blocks)).start()

    def scatter(u, first):
        return lambda d: pltpu.make_async_remote_copy(
            kv_ref.at[u, d], held[u].at[me], s1.at[u], r1.at[u], device_id={"ctx": first + d, "head": half})

    for u in range(units):
        @pl.when(lower)
        def _(u=u):
            far_all(scatter(u, side_blocks))

        near_all(scatter(u, base))

    perm[...] = pick((TILE, TILE), q_column)
    back[0] = pick((TILE, TILE), q_back)
    back[1] = pick((TILE, TILE), grad_back)
    for copy in reads:
        copy.wait()

    @pl.loop(0, rows // tokens)
    def _(i):
        at = pl.multiple_of(i * tokens, tokens)
        for e in range(2):
            y = dot_nn(perm[...], raw[e, pl.ds(pl.multiple_of(i * TILE, TILE), TILE), :]).astype(BF16)
            for n in range(kv_heads):
                for g in range(part):
                    slab = (n * part + g) * tokens
                    staged[e, n, g, pl.ds(at, tokens), :] = y[slab:slab + tokens]

    moves = []
    for e, dst in enumerate((qv, dov)):
        src = staged.at[e]
        place = dst.at[:, pl.ds(half * part, part)]
        for i in range(1, halves):
            other = lax.rem(half + i, halves)
            moves.append(pltpu.make_async_remote_copy(
                src.at[pl.ds(other * heads, heads)], place, xs.at[e, i - 1], xr.at[e, i - 1],
                device_id={"ctx": me, "head": other}))
        moves.append(pltpu.make_async_copy(src.at[pl.ds(half * heads, heads)], place, xl.at[e]))
    for move in moves:
        move.start()

    def fetch_first(u, count):
        span = pl.ds(0, count)
        return pltpu.make_async_remote_copy(
            held[u].at[span], held[u].at[span], s1.at[u], r1.at[u], device_id=here)

    def fetch_last(u):
        span = pl.ds(0, side_blocks - 1)
        return pltpu.make_async_remote_copy(
            send.at[u, span], near.at[u, :, span], s2.at[u], r2.at[u], device_id=here)

    def relay(u):
        held[u][me] = kv_ref[u, col]

        @pl.when(lower)
        def _():
            fetch_first(u, side_blocks - 1).wait_recv()

        @pl.when(upper)
        def _():
            fetch_first(u, blocks - 1).wait_recv()

        @pl.loop(0, side_blocks)
        def _(d):
            for j in range(2):
                send[u, d, j] = held[u][sel_ref[j, base + d]]

        near_all(lambda d: pltpu.make_async_remote_copy(
            send.at[u, d], near.at[u, :, col], s2.at[u], r2.at[u], device_id={"ctx": base + d, "head": half}))
        for j in range(2):
            near[u, j, col] = held[u][sel_ref[j, me]]

    def back_first(u):
        span = pl.ds(0, side_blocks - 1)
        return pltpu.make_async_remote_copy(
            dnear.at[u, :, span], arrived.at[u, span], b1.at[u], c1.at[u], device_id=here)

    def back_last(u, count):
        span = pl.ds(0, count)
        return pltpu.make_async_remote_copy(
            home.at[u, span], home.at[u, span], b2.at[u], c2.at[u], device_id=here)

    together = math.gcd(4, side_blocks)

    def collect(u):
        back_first(u).wait_recv()

        def total_of(s, first):
            def add(c, total):
                for k in range(together):
                    d = c * together + k
                    b = base + d
                    for j in range(2):
                        mine = ((sel_ref[j, b] == s) & (b > s)).astype(F32)
                        total = total + arrived[u, d, j].astype(F32) * mine
                return total

            total = lax.fori_loop(first, side_blocks // together, add, jnp.zeros((piece, size), F32))
            home[u, s] = total.astype(BF16)

        def deliver(s):
            pltpu.make_async_remote_copy(
                home.at[u, s], ret.at[u, side, col], b2.at[u], c2.at[u],
                device_id={"ctx": s, "head": half}).start()

        @pl.when(upper)
        def _():
            @pl.loop(0, side_blocks)
            def _(i):
                total_of(lax.rem(col + i, side_blocks), 0)

                @pl.when(i > 0)
                def _():
                    deliver(lax.rem(col + i - 1, side_blocks))

            deliver(lax.rem(col + side_blocks - 1, side_blocks))

        @pl.loop(1, side_blocks + 1)
        def _(i):
            d = lax.rem(col + i, side_blocks)
            total_of(base + d, (d + 1) // together)

            @pl.when(i > 1)
            def _():
                deliver(base + lax.rem(col + i - 1, side_blocks))

        ret[u, side, col] = home[u, me]

    def results(n, e):
        src, dst = (outv, dqv)[e], landed.at[e]
        made = []
        place = dst.at[half * heads + n]
        for i in range(1, halves):
            other = lax.rem(half + i, halves)
            made.append(pltpu.make_async_remote_copy(
                src.at[n, pl.ds(other * part, part)], place, ys.at[n, e, i - 1], yr.at[n, e, i - 1],
                device_id={"ctx": me, "head": other}))
        made.append(pltpu.make_async_copy(src.at[n, pl.ds(half * part, part)], place, yl.at[n, e]))
        return made

    def join(x):
        if piece % 16 == 0:
            return x.reshape(keys, size)
        return x.astype(F32).reshape(keys, size).astype(BF16)

    def place_keys(n, j, k, key, value):
        ks[n, j, k * keys:(k + 1) * keys] = key
        vs[n, j, k * keys:(k + 1) * keys] = value
        kt[n, j, k] = flip(key)
        vt[n, 0:size, j * rows + k * keys:j * rows + (k + 1) * keys] = flip(value)

    def cuts_of(t):
        return ([(j, at) for j in range(2) for at in range(0, rows, tile)]
                + [(2, at) for at in range(0, (t + 1) * tile, tile)])

    def score(n, g):
        for t in range(2):
            q_t = qt[n, g, :, t * tile:(t + 1) * tile]
            tops = [None] * 3
            for j, at in cuts_of(t):
                s = dot_nn(ks[n, j, at:at + tile, :], q_t)
                if j == 2 and at == t * tile:
                    key_at = lax.broadcasted_iota(jnp.int32, s.shape, 0)
                    query_at = lax.broadcasted_iota(jnp.int32, s.shape, 1)
                    s = jnp.where(key_at <= query_at, s, -jnp.inf)
                marks[t, j * rows + at:j * rows + at + tile, :] = s
                top = jnp.max(s, axis=0, keepdims=True)
                tops[j] = top if tops[j] is None else jnp.maximum(tops[j], top)
            top = tops[2]
            for j in range(2):
                top = jnp.maximum(top, jnp.where(visible[j], tops[j], -jnp.inf))
            peaks[t] = top * factor

    def weigh(n, g):
        for t in range(2):
            span = slice(t * tile, (t + 1) * tile)
            top = peaks[t]
            shifts = [jnp.where(visible[j], top, jnp.inf) for j in range(2)] + [top]
            out_t = jnp.zeros((size + EXTRA, tile), F32)
            for j, at in cuts_of(t):
                span_k = slice(j * rows + at, j * rows + at + tile)
                low = jnp.exp2(marks[t, span_k, :] * factor - shifts[j]).astype(BF16)
                probs[n, g, span_k, span] = low
                out_t = out_t + dot_nn(vt[n, :, span_k], low)
            inverse = 1.0 / out_t[size:size + 1]
            out_low = (out_t[0:size] * inverse).astype(BF16).astype(F32)
            do_low = (dot[n, g, :, span].astype(F32) * inverse).astype(BF16)
            do_wide = do_low.astype(F32)
            dot[n, g, :, span] = do_low
            dov[n, g, span, :] = do_wide.T.astype(BF16)
            dots[n, g, :, span] = jnp.sum(do_wide * out_low, axis=0, keepdims=True)
            outv[n, g, span, :] = out_low.T.astype(BF16)

    def gradients(n, g, low, key_t, value, span, dk_at, dv_at):
        dp = dot_nn(value, dot[n, g, :, span])
        ds = (low.astype(F32) * (dp - dots[n, g, :, span])).astype(BF16)
        dk_at[...] += dot_nn(ds, qv[n, g, span, :])
        dv_at[...] += dot_nn(low, dov[n, g, span, :])
        return dot_nn(key_t, ds)

    def chunk(n, k, g):
        every = slice(0, rows)
        total = jnp.zeros((size, rows), F32)
        for j in range(2):
            at = pl.multiple_of(k * keys, keys)
            low = probs[n, g, pl.ds(pl.multiple_of(j * rows + k * keys, keys), keys), :]
            total = total + gradients(n, g, low, kt[n, j, k], vs[n, j, pl.ds(at, keys), :], every,
                                      dk.at[j], dv.at[j])

        @pl.when(k == 0)
        def _():
            dqt[n, g] = total

        @pl.when(k > 0)
        def _():
            dqt[n, g] += total

    def own_chunk(n, g):
        total = dqt[n, g]
        tails = []
        for k in range(CHUNKS):
            span = slice(k * keys, rows)
            low = probs[n, g, 2 * rows + k * keys:2 * rows + (k + 1) * keys, span]
            at = slice(k * keys, (k + 1) * keys)
            tails.append(gradients(n, g, low, kt[n, 2, k], vs[n, 2, at, :], span, dko.at[at], dvo.at[at]))
        for t in range(CHUNKS):
            span = slice(t * keys, (t + 1) * keys)
            dq = total[:, span]
            for k in range(t + 1):
                dq = dq + tails[k][:, (t - k) * keys:(t - k + 1) * keys]
            dqv[n, g, span, :] = (dq * scale).T.astype(BF16)

    for n in range(heads):
        for k in range(CHUNKS):
            span = slice(k * keys, (k + 1) * keys)
            place_keys(n, 2, k, own_ref[n, 0, span], own_ref[n, 1, span])

    for move in moves:
        move.wait()

    @pl.loop(0, heads * group)
    def _(at):
        n, g = at // group, lax.rem(at, group)
        qt[n, g] = flip(qv[n, g])
        dot[n, g] = flip(dov[n, g])

    for u in range(CHUNKS):
        relay(u)

    @pl.loop(0, heads)
    def _(n):
        for k in range(CHUNKS):
            u = n * CHUNKS + k
            fetch_last(u).wait_recv()
            for j in range(2):
                place_keys(n, j, k, join(near[u, j, 0:pieces]), join(near[u, j, pieces:2 * pieces]))

        @pl.loop(0, 2 * group)
        def _(at):
            g = at // 2

            @pl.when(lax.rem(at, 2) == 0)
            def _():
                score(n, g)

            @pl.when(lax.rem(at, 2) == 1)
            def _():
                weigh(n, g)

            for m in range(1, heads):
                for k in range(CHUNKS):
                    @pl.when((n == m - 1) & (at == 1 + 2 * k * (group - 1)))
                    def _(m=m, k=k):
                        relay(m * CHUNKS + k)

            @pl.when((n > 0) & (lax.rem(at, 4) == 3))
            def _():
                collect((n - 1) * CHUNKS + g // 2)

        for move in results(n, 0):
            move.start()

        @pl.loop(0, CHUNKS * group)
        def _(at):
            k, g = at // group, lax.rem(at, group)
            u = n * CHUNKS + k

            @pl.when(g == 0)
            def _():
                dk[...] = jnp.zeros_like(dk)
                dv[...] = jnp.zeros_like(dv)

            chunk(n, k, g)

            @pl.when(g == group - 1)
            def _():
                for j in range(2):
                    dnear[u, j, 0:pieces] = (dk[j] * scale).reshape(pieces, piece, size).astype(BF16)
                    dnear[u, j, pieces:2 * pieces] = dv[j].reshape(pieces, piece, size).astype(BF16)
                near_all(lambda d: pltpu.make_async_remote_copy(
                    dnear.at[u, :, d], arrived.at[u, col], b1.at[u], c1.at[u],
                    device_id={"ctx": base + d, "head": half}))
                for j in range(2):
                    arrived[u, col, j] = dnear[u, j, col]

    @pl.loop(0, heads * group)
    def _(at):
        n, g = at // group, lax.rem(at, group)

        @pl.when(g == 0)
        def _():
            dko[...] = jnp.zeros_like(dko)
            dvo[...] = jnp.zeros_like(dvo)

        own_chunk(n, g)

        for k in range(CHUNKS):
            @pl.when(at == (1 + 4 * k))
            def _(k=k):
                collect((heads - 1) * CHUNKS + k)

        @pl.when(g == group - 1)
        def _():
            for k in range(CHUNKS):
                u = n * CHUNKS + k
                span = slice(k * keys, (k + 1) * keys)
                down[u, 0:pieces] = (dko[span] * scale).reshape(pieces, piece, size)
                down[u, pieces:2 * pieces] = dvo[span].reshape(pieces, piece, size)
            for move in results(n, 1):
                move.start()

    writes = []
    for e, dst in enumerate((oo_ref, dqo_ref)):
        for n in range(heads):
            for move in results(n, e):
                move.wait()

        @pl.loop(0, rows // tokens)
        def _(i, e=e):
            at = pl.multiple_of(i * tokens, tokens)
            x = jnp.concatenate([landed[e, n, g, pl.ds(at, tokens), :]
                                 for n in range(kv_heads) for g in range(part)], axis=0)
            raw[e, pl.ds(pl.multiple_of(i * TILE, TILE), TILE), :] = dot_nn(back[0], x).astype(BF16)

        writes.append(pltpu.make_async_copy(raw.at[e], dst, ol.at[e]))
        writes[e].start()

    for u in range(units):
        fetch_last(u).wait_send()
        back_first(u).wait_send()

    def finish(k, low):
        for e, dst in enumerate((gk_ref, gv_ref)):
            span = slice(e * pieces, (e + 1) * pieces)
            parts = []
            for n in range(heads):
                u = n * CHUNKS + k
                total = down[u, span] + ret[u, 1, span].astype(F32)
                if low:
                    total = total + ret[u, 0, span].astype(F32)
                parts.append(total.reshape(keys, size).astype(BF16))
            for i in range(keys // grad_tokens):
                x = jnp.concatenate([p[i * grad_tokens:(i + 1) * grad_tokens] for p in parts], axis=0)
                at = k * keys * heads + i * TILE
                dst[at:at + TILE, :] = dot_nn(back[1], x).astype(BF16)

    @pl.when(lower)
    def _():
        for u in range(units):
            fetch_first(u, blocks - 1).wait_send()
            back_last(u, side_blocks - 1).wait_send()
        for k in range(CHUNKS):
            for n in range(heads):
                back_last(n * CHUNKS + k, blocks - 1).wait_recv()
            finish(k, True)

    @pl.when(upper)
    def _():
        for u in range(units):
            fetch_first(u, side_blocks - 1).wait_send()
            back_last(u, blocks - 1).wait_send()
        for k in range(CHUNKS):
            for n in range(heads):
                back_last(n * CHUNKS + k, side_blocks - 1).wait_recv()
            finish(k, False)

    for write in writes:
        write.wait()


def step(selected, key, value, q, do, blocks, halves, rows, part):
    size = key.shape[1]
    kv_heads = key.shape[0] // rows
    heads, group = kv_heads // halves, part * halves
    units, side_blocks, keys = heads * CHUNKS, blocks // 2, rows // CHUNKS
    piece = 2 * keys // side_blocks
    near = pl.BlockSpec(memory_space=pltpu.VMEM)
    far = pl.BlockSpec(memory_space=pl.ANY)
    dma = pltpu.SemaphoreType.DMA
    vmem = pltpu.VMEM
    wide = jax.ShapeDtypeStruct(q.shape, BF16)
    grad = jax.ShapeDtypeStruct((rows * heads, size), BF16)
    return pl.pallas_call(
        functools.partial(step_kernel, blocks, halves),
        in_specs=[pl.BlockSpec(memory_space=pltpu.SMEM), far, far, far, far],
        out_specs=[far, far, near, near],
        out_shape=[wide, wide, grad, grad],
        scratch_shapes=[
            vmem((2,) + key.shape, BF16),
            vmem((2,) + q.shape, BF16),
            vmem((2, kv_heads, part, rows, size), BF16),
            vmem((heads, 2, rows, size), BF16),
            vmem((units, side_blocks, piece, size), BF16),
            vmem((TILE, TILE), BF16),
            vmem((2, TILE, TILE), BF16),
            vmem((heads, group, rows, size), BF16),
            vmem((heads, group, rows, size), BF16),
            vmem((heads, group, size, rows), BF16),
            vmem((heads, group, size, rows), BF16),
            vmem((units, 2, side_blocks, piece, size), BF16),
            vmem((units, side_blocks, 2, piece, size), BF16),
            vmem((heads, 3, rows, size), BF16),
            vmem((heads, 3, rows, size), BF16),
            vmem((heads, 3, CHUNKS, size, keys), BF16),
            vmem((heads, size + EXTRA, 3 * rows), BF16),
            vmem((2, 3 * rows, rows // 2), F32),
            vmem((2, 1, rows // 2), F32),
            vmem((heads, group, 3 * rows, rows), BF16),
            vmem((heads, group, 1, rows), F32),
            vmem((heads, group, size, rows), F32),
            vmem((2, keys, size), F32),
            vmem((2, keys, size), F32),
            vmem((rows, size), F32),
            vmem((rows, size), F32),
            vmem((units, side_blocks, piece, size), F32),
            vmem((heads, group, rows, size), BF16),
            vmem((heads, group, rows, size), BF16),
            vmem((2, kv_heads, part, rows, size), BF16),
            vmem((units, 2, side_blocks, piece, size), BF16),
            vmem((units, side_blocks, 2, piece, size), BF16),
            vmem((units, blocks, piece, size), BF16),
            vmem((units, 2, side_blocks, piece, size), BF16),
            dma((units,)), dma((units,)), dma((units,)), dma((units,)),
            dma((2,)), dma((2,)), dma((2,)), dma((2, halves - 1)), dma((2, halves - 1)), dma((2,)),
            dma((units,)), dma((units,)), dma((units,)), dma((units,)),
            dma((heads, 2, halves - 1)), dma((heads, 2, halves - 1)), dma((heads, 2)),
        ] + [vmem((blocks, piece, size), BF16)] * units,
        compiler_params=pltpu.CompilerParams(collective_id=0, has_side_effects=True,
                                             vmem_limit_bytes=56 * 2**20),
    )(selected, key, value, q, do)


def on_device(queries, keys, values, output_gradient, selected):
    rows, kv_count, size = keys.shape
    blocks, halves = lax.axis_size("ctx"), lax.axis_size("head")
    part = queries.shape[1]
    flat = [x.reshape(-1, size) for x in (keys, values, queries, output_gradient)]
    out, dq, gk, gv = step(selected.T, *flat, blocks, halves, rows, part)
    own = (rows, kv_count // halves, size)
    return out.reshape(queries.shape), dq.reshape(queries.shape), gk.reshape(own), gv.reshape(own)


def solution(mesh):
    return jax.shard_map(
        on_device,
        mesh=mesh,
        in_specs=(
            P("ctx", "head", None, None),
            P("ctx", None, None),
            P("ctx", None, None),
            P("ctx", "head", None, None),
            P(),
        ),
        out_specs=(
            P("ctx", "head", None, None),
            P("ctx", "head", None, None),
            P("ctx", "head", None),
            P("ctx", "head", None),
        ),
        check_vma=False,
    )
```

```python
import functools
import math

import jax
import jax.numpy as jnp
from jax import lax
from jax.experimental import pallas as pl
from jax.experimental.pallas import tpu as pltpu
from jax.sharding import PartitionSpec as P

F32 = jnp.float32
BF16 = jnp.bfloat16
CHUNKS = 2
EXTRA = 16
TILE = 256
PARTS = 4


def dot_nn(a, b):
    return lax.dot_general(a, b, (((1,), (0,)), ((), ())), preferred_element_type=F32)


def greet(blocks, halves):
    me, half = lax.axis_index("ctx"), lax.axis_index("head")
    barrier = pltpu.get_barrier_semaphore()

    @pl.loop(1, blocks)
    def _(i):
        pl.semaphore_signal(barrier, inc=1, device_id={"ctx": lax.rem(me + i, blocks), "head": half})

    for i in range(1, halves):
        pl.semaphore_signal(barrier, inc=1, device_id={"ctx": me, "head": lax.rem(half + i, halves)})
    return lambda: pl.semaphore_wait(barrier, blocks - 1 + halves - 1)


def pick(shape, column_of):
    row = lax.broadcasted_iota(jnp.int32, shape, 0)
    column = lax.broadcasted_iota(jnp.int32, shape, 1)
    return jnp.where(column == column_of(row), 1.0, 0.0).astype(BF16)


def split(x, size):
    bits = size.bit_length() - 1
    assert size == 1 << bits
    return lax.shift_right_logical(x, bits), lax.bitwise_and(x, size - 1)


def flip(x):
    return x.astype(F32).T.astype(BF16)


def step_kernel(blocks, halves, sel_ref, k_ref, v_ref, q_ref, do_ref, oo_ref, dqo_ref, gk_ref, gv_ref,
                kv_raw, raw, staged, own_ref, kv_ref, perm, back, qv, dov, qt, dot, near, send, ks, vs, kt, vt, marks, peaks, probs, dots, dqt, dk, dv, dko, dvo, down, outv, dqv, landed,
                dnear, arrived, home, ret,
                s1, r1, s2, r2, kl, ql, ol, xs, xr, xl, b1, c1, b2, c2, ys, yr, yl, *held):
    me, half = lax.axis_index("ctx"), lax.axis_index("head")
    heads, group, rows, size = qv.shape
    part = group // halves
    side_blocks, piece = kv_ref.shape[1], kv_ref.shape[2]
    units = heads * CHUNKS
    keys = rows // CHUNKS
    tile = rows // 2
    side, col = me // side_blocks, lax.rem(me, side_blocks)
    base = side * side_blocks
    lower, upper = side == 0, side > 0
    scale = size ** -0.5
    factor = scale * math.log2(math.e)
    visible = [sel_ref[j, me] < me for j in range(2)]
    here = {"ctx": me, "head": half}
    kv_heads = staged.shape[1]
    joined = greet(blocks, halves)

    loads = [pltpu.make_async_copy(src, kv_raw.at[e], kl.at[e]) for e, src in enumerate((k_ref, v_ref))]
    reads = [pltpu.make_async_copy(src, raw.at[e], ql.at[e]) for e, src in enumerate((q_ref, do_ref))]
    for copy in loads + reads:
        copy.start()

    kv_tokens = TILE // kv_heads
    tokens = TILE // (kv_heads * part)
    grad_tokens = TILE // heads

    def kv_column(row):
        h, t = split(row, kv_tokens)
        return t * kv_heads + half * heads + h

    def q_column(row):
        slab, t = split(row, tokens)
        n, g = split(slab, part)
        return t * (part * kv_heads) + g * kv_heads + n

    def q_back(row):
        t, slab = split(row, part * kv_heads)
        g, n = split(slab, kv_heads)
        return (n * part + g) * tokens + t

    def grad_back(row):
        t, h = split(row, heads)
        return h * grad_tokens + t

    choose = pick((heads * kv_tokens, TILE), kv_column)
    vt[:, size:size + EXTRA, :] = jnp.ones((heads, EXTRA, 3 * rows), BF16)
    for copy in loads:
        copy.wait()
    for e in range(2):
        for i in range(rows // kv_tokens):
            y = dot_nn(choose, kv_raw[e, i * TILE:(i + 1) * TILE, :]).astype(BF16)
            for h in range(heads):
                own_ref[h, e, i * kv_tokens:(i + 1) * kv_tokens] = y[h * kv_tokens:(h + 1) * kv_tokens]
    pieces = side_blocks // 2

    def cut(x):
        if piece % 16 == 0:
            return x.reshape(pieces, piece, size)
        return x.astype(F32).reshape(pieces, piece, size).astype(BF16)

    for n in range(heads):
        for k in range(CHUNKS):
            for e in range(2):
                kv_ref[n * CHUNKS + k, e * pieces:(e + 1) * pieces] = cut(own_ref[n, e, k * keys:(k + 1) * keys])
    joined()

    def near_all(make):
        @pl.loop(1, side_blocks)
        def _(i):
            make(lax.rem(col + i, side_blocks)).start()

    def far_all(make):
        @pl.loop(0, side_blocks)
        def _(i):
            make(lax.rem(col + i, side_blocks)).start()

    def scatter(u, first):
        return lambda d: pltpu.make_async_remote_copy(
            kv_ref.at[u, d], held[u].at[me], s1.at[u], r1.at[u], device_id={"ctx": first + d, "head": half})

    for u in range(units):
        near_all(scatter(u, base))

        @pl.when(lower)
        def _(u=u):
            far_all(scatter(u, side_blocks))

    perm[...] = pick((TILE, TILE), q_column)
    back[0] = pick((TILE, TILE), q_back)
    back[1] = pick((TILE, TILE), grad_back)
    for copy in reads:
        copy.wait()

    @pl.loop(0, rows // tokens)
    def _(i):
        at = pl.multiple_of(i * tokens, tokens)
        for e in range(2):
            y = dot_nn(perm[...], raw[e, pl.ds(pl.multiple_of(i * TILE, TILE), TILE), :]).astype(BF16)
            for n in range(kv_heads):
                for g in range(part):
                    slab = (n * part + g) * tokens
                    staged[e, n, g, pl.ds(at, tokens), :] = y[slab:slab + tokens]

    moves = []
    for e, dst in enumerate((qv, dov)):
        src = staged.at[e]
        place = dst.at[:, pl.ds(half * part, part)]
        for i in range(1, halves):
            other = lax.rem(half + i, halves)
            moves.append(pltpu.make_async_remote_copy(
                src.at[pl.ds(other * heads, heads)], place, xs.at[e, i - 1], xr.at[e, i - 1],
                device_id={"ctx": me, "head": other}))
        moves.append(pltpu.make_async_copy(src.at[pl.ds(half * heads, heads)], place, xl.at[e]))
    for move in moves:
        move.start()

    def fetch_first(u, count):
        span = pl.ds(0, count)
        return pltpu.make_async_remote_copy(
            held[u].at[span], held[u].at[span], s1.at[u], r1.at[u], device_id=here)

    def fetch_last(u):
        span = pl.ds(0, side_blocks - 1)
        return pltpu.make_async_remote_copy(
            send.at[u, span], near.at[u, :, span], s2.at[u], r2.at[u], device_id=here)

    def relay(u):
        held[u][me] = kv_ref[u, col]

        @pl.when(lower)
        def _():
            fetch_first(u, side_blocks - 1).wait_recv()

        @pl.when(upper)
        def _():
            fetch_first(u, blocks - 1).wait_recv()

        @pl.loop(0, side_blocks)
        def _(d):
            for j in range(2):
                send[u, d, j] = held[u][sel_ref[j, base + d]]

        near_all(lambda d: pltpu.make_async_remote_copy(
            send.at[u, d], near.at[u, :, col], s2.at[u], r2.at[u], device_id={"ctx": base + d, "head": half}))
        for j in range(2):
            near[u, j, col] = held[u][sel_ref[j, me]]

    def back_first(u):
        span = pl.ds(0, side_blocks - 1)
        return pltpu.make_async_remote_copy(
            dnear.at[u, :, span], arrived.at[u, span], b1.at[u], c1.at[u], device_id=here)

    def back_last(u, count):
        span = pl.ds(0, count)
        return pltpu.make_async_remote_copy(
            home.at[u, span], home.at[u, span], b2.at[u], c2.at[u], device_id=here)

    together = math.gcd(4, side_blocks)

    def collect(u):
        back_first(u).wait_recv()

        def total_of(s, first):
            def add(c, total):
                for k in range(together):
                    d = c * together + k
                    b = base + d
                    for j in range(2):
                        mine = ((sel_ref[j, b] == s) & (b > s)).astype(F32)
                        total = total + arrived[u, d, j].astype(F32) * mine
                return total

            total = lax.fori_loop(first, side_blocks // together, add, jnp.zeros((piece, size), F32))
            home[u, s] = total.astype(BF16)

        def deliver(s):
            pltpu.make_async_remote_copy(
                home.at[u, s], ret.at[u, side, col], b2.at[u], c2.at[u],
                device_id={"ctx": s, "head": half}).start()

        @pl.when(upper)
        def _():
            @pl.loop(0, side_blocks)
            def _(i):
                total_of(lax.rem(col + i, side_blocks), 0)

                @pl.when(i > 0)
                def _():
                    deliver(lax.rem(col + i - 1, side_blocks))

            deliver(lax.rem(col + side_blocks - 1, side_blocks))

        @pl.loop(1, side_blocks + 1)
        def _(i):
            d = lax.rem(col + i, side_blocks)
            total_of(base + d, (d + 1) // together)

            @pl.when(i > 1)
            def _():
                deliver(base + lax.rem(col + i - 1, side_blocks))

        ret[u, side, col] = home[u, me]

    def results(n, e):
        src, dst = (outv, dqv)[e], landed.at[e]
        made = []
        place = dst.at[half * heads + n]
        for i in range(1, halves):
            other = lax.rem(half + i, halves)
            made.append(pltpu.make_async_remote_copy(
                src.at[n, pl.ds(other * part, part)], place, ys.at[n, e, i - 1], yr.at[n, e, i - 1],
                device_id={"ctx": me, "head": other}))
        made.append(pltpu.make_async_copy(src.at[n, pl.ds(half * part, part)], place, yl.at[n, e]))
        return made

    def join(x):
        if piece % 16 == 0:
            return x.reshape(keys, size)
        return x.astype(F32).reshape(keys, size).astype(BF16)

    def place_keys(n, j, k, key, value):
        ks[n, j, k * keys:(k + 1) * keys] = key
        vs[n, j, k * keys:(k + 1) * keys] = value
        kt[n, j, k] = flip(key)
        vt[n, 0:size, j * rows + k * keys:j * rows + (k + 1) * keys] = flip(value)

    def cuts_of(t):
        return ([(j, at) for j in range(2) for at in range(0, rows, tile)]
                + [(2, at) for at in range(0, (t + 1) * tile, tile)])

    def score(n, g):
        for t in range(2):
            q_t = qt[n, g, :, t * tile:(t + 1) * tile]
            tops = [None] * 3
            for j, at in cuts_of(t):
                s = dot_nn(ks[n, j, at:at + tile, :], q_t)
                if j == 2 and at == t * tile:
                    key_at = lax.broadcasted_iota(jnp.int32, s.shape, 0)
                    query_at = lax.broadcasted_iota(jnp.int32, s.shape, 1)
                    s = jnp.where(key_at <= query_at, s, -jnp.inf)
                marks[t, j * rows + at:j * rows + at + tile, :] = s
                top = jnp.max(s, axis=0, keepdims=True)
                tops[j] = top if tops[j] is None else jnp.maximum(tops[j], top)
            top = tops[2]
            for j in range(2):
                top = jnp.maximum(top, jnp.where(visible[j], tops[j], -jnp.inf))
            peaks[t] = top * factor

    def weigh(n, g):
        for t in range(2):
            span = slice(t * tile, (t + 1) * tile)
            top = peaks[t]
            shifts = [jnp.where(visible[j], top, jnp.inf) for j in range(2)] + [top]
            out_t = jnp.zeros((size + EXTRA, tile), F32)
            for j, at in cuts_of(t):
                span_k = slice(j * rows + at, j * rows + at + tile)
                low = jnp.exp2(marks[t, span_k, :] * factor - shifts[j]).astype(BF16)
                probs[n, g, span_k, span] = low
                out_t = out_t + dot_nn(vt[n, :, span_k], low)
            inverse = 1.0 / out_t[size:size + 1]
            out_low = (out_t[0:size] * inverse).astype(BF16).astype(F32)
            do_low = (dot[n, g, :, span].astype(F32) * inverse).astype(BF16)
            do_wide = do_low.astype(F32)
            dot[n, g, :, span] = do_low
            dov[n, g, span, :] = do_wide.T.astype(BF16)
            dots[n, g, :, span] = jnp.sum(do_wide * out_low, axis=0, keepdims=True)
            outv[n, g, span, :] = out_low.T.astype(BF16)

    def gradients(n, g, low, key_t, value, span, dk_at, dv_at):
        dp = dot_nn(value, dot[n, g, :, span])
        ds = (low.astype(F32) * (dp - dots[n, g, :, span])).astype(BF16)
        dk_at[...] += dot_nn(ds, qv[n, g, span, :])
        dv_at[...] += dot_nn(low, dov[n, g, span, :])
        return dot_nn(key_t, ds)

    def chunk(n, k, g):
        every = slice(0, rows)
        total = jnp.zeros((size, rows), F32)
        for j in range(2):
            at = pl.multiple_of(k * keys, keys)
            low = probs[n, g, pl.ds(pl.multiple_of(j * rows + k * keys, keys), keys), :]
            total = total + gradients(n, g, low, kt[n, j, k], vs[n, j, pl.ds(at, keys), :], every,
                                      dk.at[j], dv.at[j])

        @pl.when(k == 0)
        def _():
            dqt[n, g] = total

        @pl.when(k > 0)
        def _():
            dqt[n, g] += total

    def own_chunk(n, g):
        total = dqt[n, g]
        tails = []
        for k in range(CHUNKS):
            span = slice(k * keys, rows)
            low = probs[n, g, 2 * rows + k * keys:2 * rows + (k + 1) * keys, span]
            at = slice(k * keys, (k + 1) * keys)
            tails.append(gradients(n, g, low, kt[n, 2, k], vs[n, 2, at, :], span, dko.at[at], dvo.at[at]))
        for t in range(CHUNKS):
            span = slice(t * keys, (t + 1) * keys)
            dq = total[:, span]
            for k in range(t + 1):
                dq = dq + tails[k][:, (t - k) * keys:(t - k + 1) * keys]
            dqv[n, g, span, :] = (dq * scale).T.astype(BF16)

    for n in range(heads):
        for k in range(CHUNKS):
            span = slice(k * keys, (k + 1) * keys)
            place_keys(n, 2, k, own_ref[n, 0, span], own_ref[n, 1, span])

    for move in moves:
        move.wait()

    @pl.loop(0, heads * group)
    def _(at):
        n, g = at // group, lax.rem(at, group)
        qt[n, g] = flip(qv[n, g])
        dot[n, g] = flip(dov[n, g])

    for u in range(CHUNKS):
        relay(u)

    @pl.loop(0, heads)
    def _(n):
        for k in range(CHUNKS):
            u = n * CHUNKS + k
            fetch_last(u).wait_recv()
            for j in range(2):
                place_keys(n, j, k, join(near[u, j, 0:pieces]), join(near[u, j, pieces:2 * pieces]))

        @pl.loop(0, 2 * group)
        def _(at):
            g = at // 2

            @pl.when(lax.rem(at, 2) == 0)
            def _():
                score(n, g)

            @pl.when(lax.rem(at, 2) == 1)
            def _():
                weigh(n, g)

            for m in range(1, heads):
                for k in range(CHUNKS):
                    @pl.when((n == m - 1) & (at == 1 + 2 * k * (group - 1)))
                    def _(m=m, k=k):
                        relay(m * CHUNKS + k)

            @pl.when((n > 0) & (lax.rem(at, 4) == 3))
            def _():
                collect((n - 1) * CHUNKS + g // 2)

        for move in results(n, 0):
            move.start()

        @pl.loop(0, CHUNKS * group)
        def _(at):
            k, g = at // group, lax.rem(at, group)
            u = n * CHUNKS + k

            @pl.when(g == 0)
            def _():
                dk[...] = jnp.zeros_like(dk)
                dv[...] = jnp.zeros_like(dv)

            chunk(n, k, g)

            @pl.when(g == group - 1)
            def _():
                for j in range(2):
                    dnear[u, j, 0:pieces] = (dk[j] * scale).reshape(pieces, piece, size).astype(BF16)
                    dnear[u, j, pieces:2 * pieces] = dv[j].reshape(pieces, piece, size).astype(BF16)
                near_all(lambda d: pltpu.make_async_remote_copy(
                    dnear.at[u, :, d], arrived.at[u, col], b1.at[u], c1.at[u],
                    device_id={"ctx": base + d, "head": half}))
                for j in range(2):
                    arrived[u, col, j] = dnear[u, j, col]

    @pl.loop(0, heads * group)
    def _(at):
        n, g = at // group, lax.rem(at, group)

        @pl.when(g == 0)
        def _():
            dko[...] = jnp.zeros_like(dko)
            dvo[...] = jnp.zeros_like(dvo)

        own_chunk(n, g)

        for k in range(CHUNKS):
            @pl.when(at == (1 + 4 * k))
            def _(k=k):
                collect((heads - 1) * CHUNKS + k)

        @pl.when(g == group - 1)
        def _():
            for k in range(CHUNKS):
                u = n * CHUNKS + k
                span = slice(k * keys, (k + 1) * keys)
                down[u, 0:pieces] = (dko[span] * scale).reshape(pieces, piece, size)
                down[u, pieces:2 * pieces] = dvo[span].reshape(pieces, piece, size)
            for move in results(n, 1):
                move.start()

    writes = []
    for e, dst in enumerate((oo_ref, dqo_ref)):
        for n in range(heads):
            for move in results(n, e):
                move.wait()

        @pl.loop(0, rows // tokens)
        def _(i, e=e):
            at = pl.multiple_of(i * tokens, tokens)
            x = jnp.concatenate([landed[e, n, g, pl.ds(at, tokens), :]
                                 for n in range(kv_heads) for g in range(part)], axis=0)
            raw[e, pl.ds(pl.multiple_of(i * TILE, TILE), TILE), :] = dot_nn(back[0], x).astype(BF16)

        writes.append(pltpu.make_async_copy(raw.at[e], dst, ol.at[e]))
        writes[e].start()

    for u in range(units):
        fetch_last(u).wait_send()
        back_first(u).wait_send()

    def finish(k, low):
        for e, dst in enumerate((gk_ref, gv_ref)):
            span = slice(e * pieces, (e + 1) * pieces)
            parts = []
            for n in range(heads):
                u = n * CHUNKS + k
                total = down[u, span] + ret[u, 1, span].astype(F32)
                if low:
                    total = total + ret[u, 0, span].astype(F32)
                parts.append(total.reshape(keys, size).astype(BF16))
            for i in range(keys // grad_tokens):
                x = jnp.concatenate([p[i * grad_tokens:(i + 1) * grad_tokens] for p in parts], axis=0)
                at = k * keys * heads + i * TILE
                dst[at:at + TILE, :] = dot_nn(back[1], x).astype(BF16)

    @pl.when(lower)
    def _():
        for u in range(units):
            fetch_first(u, blocks - 1).wait_send()
            back_last(u, side_blocks - 1).wait_send()
        for k in range(CHUNKS):
            for n in range(heads):
                back_last(n * CHUNKS + k, blocks - 1).wait_recv()
            finish(k, True)

    @pl.when(upper)
    def _():
        for u in range(units):
            fetch_first(u, side_blocks - 1).wait_send()
            back_last(u, blocks - 1).wait_send()
        for k in range(CHUNKS):
            for n in range(heads):
                back_last(n * CHUNKS + k, side_blocks - 1).wait_recv()
            finish(k, False)

    for write in writes:
        write.wait()


def step(selected, key, value, q, do, blocks, halves, rows, part):
    size = key.shape[1]
    kv_heads = key.shape[0] // rows
    heads, group = kv_heads // halves, part * halves
    units, side_blocks, keys = heads * CHUNKS, blocks // 2, rows // CHUNKS
    piece = 2 * keys // side_blocks
    near = pl.BlockSpec(memory_space=pltpu.VMEM)
    far = pl.BlockSpec(memory_space=pl.ANY)
    dma = pltpu.SemaphoreType.DMA
    vmem = pltpu.VMEM
    wide = jax.ShapeDtypeStruct(q.shape, BF16)
    grad = jax.ShapeDtypeStruct((rows * heads, size), BF16)
    return pl.pallas_call(
        functools.partial(step_kernel, blocks, halves),
        in_specs=[pl.BlockSpec(memory_space=pltpu.SMEM), far, far, far, far],
        out_specs=[far, far, near, near],
        out_shape=[wide, wide, grad, grad],
        scratch_shapes=[
            vmem((2,) + key.shape, BF16),
            vmem((2,) + q.shape, BF16),
            vmem((2, kv_heads, part, rows, size), BF16),
            vmem((heads, 2, rows, size), BF16),
            vmem((units, side_blocks, piece, size), BF16),
            vmem((TILE, TILE), BF16),
            vmem((2, TILE, TILE), BF16),
            vmem((heads, group, rows, size), BF16),
            vmem((heads, group, rows, size), BF16),
            vmem((heads, group, size, rows), BF16),
            vmem((heads, group, size, rows), BF16),
            vmem((units, 2, side_blocks, piece, size), BF16),
            vmem((units, side_blocks, 2, piece, size), BF16),
            vmem((heads, 3, rows, size), BF16),
            vmem((heads, 3, rows, size), BF16),
            vmem((heads, 3, CHUNKS, size, keys), BF16),
            vmem((heads, size + EXTRA, 3 * rows), BF16),
            vmem((2, 3 * rows, rows // 2), F32),
            vmem((2, 1, rows // 2), F32),
            vmem((heads, group, 3 * rows, rows), BF16),
            vmem((heads, group, 1, rows), F32),
            vmem((heads, group, size, rows), F32),
            vmem((2, keys, size), F32),
            vmem((2, keys, size), F32),
            vmem((rows, size), F32),
            vmem((rows, size), F32),
            vmem((units, side_blocks, piece, size), F32),
            vmem((heads, group, rows, size), BF16),
            vmem((heads, group, rows, size), BF16),
            vmem((2, kv_heads, part, rows, size), BF16),
            vmem((units, 2, side_blocks, piece, size), BF16),
            vmem((units, side_blocks, 2, piece, size), BF16),
            vmem((units, blocks, piece, size), BF16),
            vmem((units, 2, side_blocks, piece, size), BF16),
            dma((units,)), dma((units,)), dma((units,)), dma((units,)),
            dma((2,)), dma((2,)), dma((2,)), dma((2, halves - 1)), dma((2, halves - 1)), dma((2,)),
            dma((units,)), dma((units,)), dma((units,)), dma((units,)),
            dma((heads, 2, halves - 1)), dma((heads, 2, halves - 1)), dma((heads, 2)),
        ] + [vmem((blocks, piece, size), BF16)] * units,
        compiler_params=pltpu.CompilerParams(collective_id=0, has_side_effects=True,
                                             vmem_limit_bytes=56 * 2**20),
    )(selected, key, value, q, do)


def hand_out_kernel(*refs):
    count = (len(refs) - 2) // 3
    sources, targets, held = refs[:count], refs[count:2 * count], refs[2 * count:3 * count]
    into, out = refs[3 * count:]
    pieces = []
    for e in range(count):
        step_rows = held[e].shape[0] // PARTS
        for p in range(PARTS):
            span = pl.ds(p * step_rows, step_rows)
            pieces.append((pltpu.make_async_copy(sources[e].at[span], held[e].at[span], into.at[e, p]),
                           pltpu.make_async_copy(held[e].at[span], targets[e].at[span], out.at[e, p])))
    for first, _ in pieces:
        first.start()
    for first, second in pieces:
        first.wait()
        second.start()
    for _, second in pieces:
        second.wait()


def hand_out(arrays):
    far = pl.BlockSpec(memory_space=pl.ANY)
    count = len(arrays)
    return pl.pallas_call(
        hand_out_kernel,
        in_specs=[far] * count,
        out_specs=[far] * count,
        out_shape=[jax.ShapeDtypeStruct(x.shape, x.dtype) for x in arrays],
        scratch_shapes=[pltpu.VMEM(x.shape, x.dtype) for x in arrays]
        + [pltpu.SemaphoreType.DMA((count, PARTS))] * 2,
        compiler_params=pltpu.CompilerParams(vmem_limit_bytes=60 * 2**20),
    )(*arrays)


def on_device(queries, keys, values, output_gradient, selected):
    rows, kv_count, size = keys.shape
    blocks, halves = lax.axis_size("ctx"), lax.axis_size("head")
    part = queries.shape[1]
    flat = [x.reshape(-1, size) for x in (keys, values, queries, output_gradient)]
    out, dq, gk, gv = hand_out(step(selected.T, *flat, blocks, halves, rows, part))
    own = (rows, kv_count // halves, size)
    return out.reshape(queries.shape), dq.reshape(queries.shape), gk.reshape(own), gv.reshape(own)


def solution(mesh):
    return jax.shard_map(
        on_device,
        mesh=mesh,
        in_specs=(
            P("ctx", "head", None, None),
            P("ctx", None, None),
            P("ctx", None, None),
            P("ctx", "head", None, None),
            P(),
        ),
        out_specs=(
            P("ctx", "head", None, None),
            P("ctx", "head", None, None),
            P("ctx", "head", None),
            P("ctx", "head", None),
        ),
        check_vma=False,
    )
```
